32 devices in a mesh: row: 8 (over z, x), col: 4 (over y, core).
Axes of the slice: x: 2, y: 2, z: 4, core: 2. Of those that a mesh axis runs over, the one named last changes fastest.
Arguments:
- panel: float32 [8, 16384, 4, 1024], P('row', None, 'col'), may hold values from -1 to 4, as said below
- rhs: float32 [8, 16384, 256], P('row'), may hold values from -6 to 6
Outputs:
- solved: float32 [4, 1024, 256], P('col')
- remainder: float32 [8, 16384, 256], P('row', None, 'col')
The draws below stay inside these ranges and needn't reach their ends.
Inputs may be any that keep to these rules, and one draw needn't show every extreme that they name: panel is lower triangular in the global indices: entries with column above row are zero, diagonal entries lie between 2 and 4, the others are of size about 1 / sqrt(4096).
All inputs are finite; a program needn't handle non-finite values.
Results may differ from the reference program's by a relative error of at most 0.000084.
Values sent between devices are 32-bit elements; how exact they have to be, the bound alone decides.
A program may use at most 256 MiB of HBM per device.

```python
import math
import jax
import jax.numpy as jnp
from jax import lax

ORDER = 131072
TB = 512
STEPS = 8
RHS = 256
ROW_CLASSES = 8
COL_CLASSES = 4
RT_DEV = 32
CT_DEV = 2


def draw_panel(key, part):
    array_shape = (ROW_CLASSES, RT_DEV * TB, COL_CLASSES, CT_DEV * TB)
    row_class = lax.broadcasted_iota(jnp.int32, array_shape, 0)
    row_inner = lax.broadcasted_iota(jnp.int32, array_shape, 1)
    col_class = lax.broadcasted_iota(jnp.int32, array_shape, 2)
    col_inner = lax.broadcasted_iota(jnp.int32, array_shape, 3)
    global_row = (row_inner // TB * ROW_CLASSES + row_class) * TB + row_inner % TB
    global_col = (col_inner // TB * COL_CLASSES + col_class) * TB + col_inner % TB
    key_off = jax.random.fold_in(key, 11)
    key_diag = jax.random.fold_in(key, 23)
    off_diag = jnp.clip(jax.random.normal(key_off, array_shape, jnp.float32), -6.0, 6.0)
    same_tile = (global_row // TB == global_col // TB).astype(jnp.float32)
    below_tile = (global_row // TB == global_col // TB + 1).astype(jnp.float32)
    off_diag = (off_diag + 0.3 * same_tile + 0.45 * below_tile) / math.sqrt(STEPS * TB)
    diag_vals = jax.random.uniform(key_diag, array_shape, jnp.float32, 2.0, 4.0)
    entries = jnp.where(global_col > global_row, 0.0, jnp.where(global_col == global_row, diag_vals, off_diag))
    return entries.astype(jnp.float32)


def shard_levels(rng, dims, split, least, high):
    def one(dim, blocks):
        draws = jax.random.uniform(jax.random.fold_in(jax.random.fold_in(rng, 6), dim), (blocks,), jnp.float32, least / len(split), high / len(split))
        return jnp.repeat(jnp.exp(draws), dims[dim] // blocks).reshape((-1,) + (1,) * (len(dims) - dim - 1))

    gain = one(*split[0])
    for cut in split[1:]:
        gain = gain * one(*cut)
    return gain


def centred(rng, extent, scale, limit, shards=(), dtype=jnp.bfloat16):
    array = scale * jax.random.normal(rng, extent, jnp.float32)
    if shards:
        array = array * shard_levels(rng, extent, shards, -0.22, 0.18)
    return jnp.clip(array, -limit, limit).astype(dtype)


def setup_inputs(seed: int = 0) -> dict:
    seeds = jax.random.split(jax.random.key(seed), 3)
    return {
        "panel": draw_panel(jax.random.fold_in(seeds[2], 71), 0),
        "rhs": centred(seeds[1], (ROW_CLASSES, RT_DEV * TB, RHS), 1.0, 6.0, ((0, 8),), jnp.float32),
    }


def reference(panel, rhs):
    window = STEPS * TB
    full_panel = panel.reshape(ROW_CLASSES, RT_DEV, TB, COL_CLASSES, CT_DEV, TB)
    full_panel = full_panel.transpose(1, 0, 2, 4, 3, 5).reshape(ORDER, window)
    right_side = rhs.reshape(ROW_CLASSES, RT_DEV, TB, RHS).transpose(1, 0, 2, 3).reshape(ORDER, RHS)
    solved = lax.linalg.triangular_solve(full_panel[:window], right_side[:window], left_side=True, lower=True)
    remainder = right_side - jnp.dot(full_panel.astype(jnp.float32), solved.astype(jnp.float32), precision=lax.Precision.HIGHEST, preferred_element_type=jnp.float32)
    laid_out = remainder.reshape(RT_DEV, ROW_CLASSES, TB, RHS).transpose(1, 0, 2, 3).reshape(ROW_CLASSES, RT_DEV * TB, RHS)
    solved_out = solved.reshape(CT_DEV, COL_CLASSES, TB, RHS).transpose(1, 0, 2, 3).reshape(COL_CLASSES, CT_DEV * TB, RHS)
    return (solved_out, laid_out)
```

```python
import jax
import jax.numpy as jnp
from jax import lax
from jax.sharding import PartitionSpec as P

TB = 512
BASE = 128
CHUNKS = 4
LANES = 128


def dot(left, right, precision=lax.Precision.HIGHEST):
    return jnp.matmul(left, right, precision=precision, preferred_element_type=jnp.float32)


def invert_lower(tile):
    size = tile.shape[0]
    count = size // BASE
    blocks = jnp.stack(
        [tile[i * BASE : (i + 1) * BASE, i * BASE : (i + 1) * BASE] for i in range(count)]
    )
    eye = jnp.eye(BASE, dtype=jnp.float32)
    scale = 1.0 / jnp.sum(blocks * eye, axis=2)
    power = -jnp.tril(blocks * scale[:, :, None], -1)
    inverse = eye + power
    reach = 2
    while reach < BASE:
        power = dot(power, power)
        inverse = inverse + dot(inverse, power)
        reach *= 2
    inverse = inverse * scale[:, None, :]
    parts = [inverse[i] for i in range(count)]
    width = BASE
    while len(parts) > 1:
        merged = []
        for i in range(0, len(parts), 2):
            lo = i * width
            below = tile[lo + width : lo + 2 * width, lo : lo + width]
            corner = -dot(parts[i + 1], dot(below, parts[i]))
            top = jnp.concatenate([parts[i], jnp.zeros_like(corner)], 1)
            merged.append(jnp.concatenate([top, jnp.concatenate([corner, parts[i + 1]], 1)], 0))
        parts = merged
        width *= 2
    return parts[0]


def pack(value, factor):
    rows = value.shape[0] // factor
    return jnp.concatenate([value[i * rows : (i + 1) * rows] for i in range(factor)], 1)


def unpack(value, factor):
    width = value.shape[1] // factor
    return jnp.concatenate([value[:, i * width : (i + 1) * width] for i in range(factor)], 0)


def on_device(panel, rhs):
    col_count = lax.axis_size("col")
    here_row = lax.axis_index("row")
    here_col = lax.axis_index("col")
    local_panel = panel.reshape(panel.shape[1], panel.shape[3])
    right_side = rhs.reshape(rhs.shape[1], rhs.shape[2])
    rows, width = right_side.shape
    tile_cols = local_panel.shape[1] // TB
    steps = tile_cols * col_count

    top = local_panel[:TB]
    diag_col = jnp.minimum(here_row // col_count, tile_cols - 1)
    has_diag = jnp.logical_and(here_row < steps, here_row % col_count == here_col)
    picked = lax.dynamic_slice_in_dim(top, diag_col * TB, TB, 1)
    diag = lax.psum(jnp.where(has_diag, picked, 0.0), "col")
    diag = jnp.where(here_row < steps, diag, jnp.eye(TB, dtype=jnp.float32))
    inverse = invert_lower(diag)
    tile_of = (jnp.arange(tile_cols * TB) // TB) * col_count + here_col
    coupling = dot(inverse, jnp.where((tile_of < here_row)[None, :], top, 0.0))
    direct = jnp.where(has_diag, dot(inverse, right_side[:TB]), 0.0)

    own = [jnp.zeros((TB, width), jnp.float32) for _ in range(tile_cols)]
    for step in range(steps):
        term = direct
        known = -(-step // col_count)
        if known:
            stacked = own[0] if known == 1 else jnp.concatenate(own[:known], 0)
            term = direct - dot(coupling[:, : known * TB], stacked)
        block = lax.psum(jnp.where(here_row == step, term, 0.0), ("row", "col"))
        place = step // col_count
        own[place] = jnp.where(here_col == step % col_count, block, own[place])
    own_solved = own[0] if tile_cols == 1 else jnp.concatenate(own, 0)

    chips = col_count // 2
    part = width // col_count
    half = width // 2
    factor = max(1, LANES // part)
    chip = here_col // 2
    core = here_col % 2

    def columns(target_core, hop):
        target = lax.rem(chip - 1 - hop + 2 * chips, chips) * 2 + target_core
        return lax.dynamic_slice_in_dim(own_solved, target * part, part, 1)

    order = [columns(1 - core, hop) for hop in range(chips)]
    order += [columns(core, hop) for hop in range(chips)]
    weights = jnp.concatenate(order, 1)
    swap = [(c, c ^ 1) for c in range(col_count)]
    ring = [(c, (c + 2) % col_count) for c in range(col_count)]
    size = rows // CHUNKS
    pieces = []
    for chunk in range(CHUNKS):
        lo = chunk * size
        product = dot(local_panel[lo : lo + size], weights, lax.Precision.HIGH)
        paired = product[:, half:] + lax.ppermute(product[:, :half], "col", swap)
        total = pack(paired[:, :part], factor)
        for hop in range(1, chips):
            total = lax.ppermute(total, "col", ring)
            total = total + pack(paired[:, hop * part : (hop + 1) * part], factor)
        mine = lax.dynamic_slice(right_side, (lo, here_col * part), (size, part))
        pieces.append(mine - unpack(total, factor))
    remainder = jnp.concatenate(pieces, 0)
    return own_solved[None], remainder[None]


def solution(mesh):
    return jax.shard_map(
        on_device,
        mesh=mesh,
        in_specs=(P("row", None, "col", None), P("row", None, None)),
        out_specs=(P("col", None, None), P("row", None, "col")),
        check_vma=False,
    )
```
